1024 devices in a mesh: row: 8 (over x, core), col: 128 (over z, y).
Axes of the slice: x: 4, y: 4, z: 32, core: 2. Of those that a mesh axis runs over, the one named last changes fastest.
Arguments:
- features: bfloat16 [65536, 256], P(('row', 'col')), may hold values from -6 to 6
- adj_tiles: bfloat16 [8, 128, 96, 128, 128], P('row', 'col'), may hold values from -0.0546875 to 0.0546875
- tile_coord: int32 [8, 128, 96], P('row', 'col'), may hold values from 0 to 255, as said below
- tile_count: int32 [8, 128], P('row', 'col'), may hold values from 1 to 96, as said below
- weight: bfloat16 [256, 256], replicated, may hold values from -0.375 to 0.375
Outputs:
- out: bfloat16 [65536, 256], P(('col', 'row'))
The draws below stay inside these ranges and needn't reach their ends.
Inputs may be any that keep to these rules, and one draw needn't show every extreme that they name: `tile_coord`: each entry is t * 64 + s for a target tile t and a source tile s; within one device's list all entries differ. `tile_count`: slots from this number on are not part of the adjacency.
All inputs are finite; a program needn't handle non-finite values.
Results may differ from the reference program's by a relative error of at most 0.0049.
Values may be sent and summed in bfloat16 or wider, within the bound.
No kernel may reach another device: no remote copies, remote signals or barrier semaphores. Data moves between devices by JAX's collectives and lax.ppermute only.
A program may use at most 128 MiB of HBM per device.

```python
import jax
import jax.numpy as jnp
from jax import lax

F = 256
TILE = 128
TGT_TILES = 4
SRC_TILES = 64
SLOTS = 96
NODES = 65536
N_ROW = 8
N_COL = 128


def draw_tile_coord(key, part):
    keys = jax.random.split(key, N_ROW * N_COL)

    def one_device(single):
        return jax.random.permutation(single, TGT_TILES * SRC_TILES)[:SLOTS].astype(jnp.int32)
    return jax.vmap(one_device)(keys).reshape(N_ROW, N_COL, SLOTS)


def draw_tile_count(key, part):
    total = N_ROW * N_COL
    counts = jax.random.randint(key, (total,), 1, SLOTS + 1).astype(jnp.int32)
    first = jax.random.randint(jax.random.fold_in(key, 11), (), 0, total)
    counts = counts.at[first].set(SLOTS)
    counts = counts.at[(first + 1) % total].set(1)
    return counts.reshape(N_ROW, N_COL)


def steps_of(own_key, dims, cuts, least, high):
    loudness, own = 1.0, jax.random.fold_in(own_key, 6)
    for axis_at, shards_of in cuts:
        draws = jnp.exp(jax.random.uniform(jax.random.fold_in(own, axis_at), (shards_of,), jnp.float32, least / len(cuts), high / len(cuts)))
        loudness = loudness * jnp.repeat(draws, dims[axis_at] // shards_of).reshape([-1 if axis == axis_at else 1 for axis in range(len(dims))])
    return loudness


def centred(stream_key, shape, deviation, reach, shards=(), kind=jnp.bfloat16):
    values = jax.random.normal(stream_key, shape, jnp.float32) * deviation
    if len(shards) > 0:
        values = steps_of(stream_key, shape, shards, -0.22, 0.18) * values
    return jnp.clip(values, min=-reach, max=reach).astype(kind)


def setup_inputs(seed: int = 0) -> dict:
    seeds = jax.random.split(jax.random.key(seed), 6)
    features = centred(seeds[0], (NODES, F), 1.0, 6.0, ((0, 1024),))
    adj_tiles = centred(seeds[1], (N_ROW, N_COL, SLOTS, TILE, TILE), (max(1, SLOTS * N_ROW * TILE // (2 * TGT_TILES))) ** -0.5, 0.0546875, ((0, 8), (1, 128)))
    tile_coord = draw_tile_coord(jax.random.fold_in(seeds[5], 71), 0)
    tile_count = draw_tile_count(jax.random.fold_in(seeds[5], 71), 0)
    weight = centred(seeds[4], (F, F), F ** -0.5, 0.375)
    return dict(features=features, adj_tiles=adj_tiles, tile_coord=tile_coord, tile_count=tile_count, weight=weight)


def device_partial(source_tiles, tile_vals, coord_list, live_count):
    live_mask = (jnp.arange(SLOTS) < live_count).astype(jnp.float32)
    target = coord_list // SRC_TILES
    source = coord_list % SRC_TILES
    feat_rows = source_tiles[source]
    products = jnp.einsum("kij,kjf->kif", tile_vals.astype(jnp.float32), feat_rows, precision=lax.Precision.HIGHEST)
    select = (target[:, None] == jnp.arange(TGT_TILES)[None, :]).astype(jnp.float32) * live_mask[:, None]
    partial_value = jnp.einsum("kt,kif->tif", select, products, precision=lax.Precision.HIGHEST)
    return partial_value.reshape(TGT_TILES * TILE, F)


def reference(features, adj_tiles, tile_coord, tile_count, weight):
    grouped = features.reshape(N_ROW, SRC_TILES, TILE, F)

    def per_row(total, inputs):
        row_feats, row_tiles, row_coords, row_counts = inputs
        source_tiles = row_feats.astype(jnp.float32)
        parts = lax.map(lambda item: device_partial(source_tiles, item[0], item[1], item[2]), (row_tiles, row_coords, row_counts))
        return total + parts, None

    start = jnp.zeros((N_COL, TGT_TILES * TILE, F), jnp.float32)
    total, unused = lax.scan(per_row, start, (grouped, adj_tiles, tile_coord, tile_count))
    hidden = total.reshape(NODES, F).astype(jnp.bfloat16)
    mixed = jnp.dot(hidden, weight, preferred_element_type=jnp.float32)
    return jax.nn.relu(mixed).astype(jnp.bfloat16)
```

```python
import functools

import jax
import jax.numpy as jnp
from jax import lax
from jax.experimental import pallas as pl
from jax.experimental.pallas import tpu as pltpu
from jax.sharding import Mesh, PartitionSpec as P

Y_RING = 4


def ring_shift(value, axis, step):
    size = lax.axis_size(axis)
    return lax.ppermute(value, axis, [(i, (i + step) % size) for i in range(size)])


def trade_halves(value, axis):
    half = value.shape[0] // 2
    return ring_shift(value[:half], axis, 1), ring_shift(value[half:], axis, -1)


def gather_ring(value):
    half = value.shape[0] // 2
    previous = ring_shift(value, "y", 1)
    following = ring_shift(value, "y", -1)
    return (
        previous,
        following,
        ring_shift(previous[:half], "y", 1),
        ring_shift(following[half:], "y", -1),
    )


def aggregate_kernel(
    place_ref, coord_ref, count_ref, adj_ref, *refs, pieces, source_count, tile
):
    piece_refs = refs[: len(pieces)]
    out_ref, dense, feats, tile_sem, feat_sem = refs[len(pieces) :]
    own_half, own_y = place_ref[0], place_ref[1]
    copies = []
    for index, (ref, (other, offset, start, length)) in enumerate(zip(piece_refs, pieces)):
        half = (own_half + other) % 2
        ring_at = (own_y + offset) % Y_RING
        copy = pltpu.make_async_copy(
            ref, feats.at[pl.ds(start, length), half, ring_at], feat_sem.at[index]
        )
        copy.start()
        copies.append(copy)

    def clear(index, carry):
        dense[index] = jnp.zeros(dense.shape[1:], dense.dtype)
        return carry

    lax.fori_loop(0, source_count, clear, 0)
    live = count_ref[0]

    def place(slot, carry):
        target = coord_ref[slot] // source_count
        source = coord_ref[slot] % source_count
        rows = pl.ds(pl.multiple_of(target * tile, tile), tile)
        pltpu.make_async_copy(adj_ref.at[slot], dense.at[source, rows], tile_sem).start()
        return carry

    lax.fori_loop(0, live, place, 0)

    def arrived(slot, carry):
        pltpu.make_async_copy(adj_ref.at[0], dense.at[0, pl.ds(0, tile)], tile_sem).wait()
        return carry

    lax.fori_loop(0, live, arrived, 0)
    for copy in copies:
        copy.wait()
    per_step = 4
    depth = feats.shape[2] * feats.shape[3]
    width = depth // tile

    def multiply(step, carry):
        left = jnp.concatenate(
            [dense[step * per_step * width + i] for i in range(per_step * width)], axis=1
        )
        right = feats[pl.ds(step * (per_step // 2), per_step // 2)]
        right = right.reshape(per_step * depth, feats.shape[-1])
        product = jnp.dot(left, right, preferred_element_type=jnp.float32)

        @pl.when(step == 0)
        def first():
            out_ref[...] = product

        @pl.when(step > 0)
        def later():
            out_ref[...] += product

        return carry

    lax.fori_loop(0, source_count // (per_step * width), multiply, 0)


def on_device(features, adj_tiles, tile_coord, tile_count, weight):
    tile = adj_tiles.shape[-1]
    rows, width = features.shape
    slots = adj_tiles.shape[2]
    z_size, y_size = lax.axis_size("z"), lax.axis_size("y")
    row_size = lax.axis_size("row")
    target_count = rows * row_size // tile
    source_count = rows * z_size * y_size // tile
    half_z = z_size // 2
    groups = [[i + 2 * j for j in range(half_z)] for i in range(2)]
    own = lax.all_gather(features, "z", axis=0, axis_index_groups=groups)
    other = jnp.concatenate(trade_halves(own, "z"), axis=0)
    arrays, pieces = [own, other], [(0, 0, 0, half_z), (1, 0, 0, half_z)]
    for which, value in ((0, own), (1, other)):
        previous, following, first, second = gather_ring(value)
        arrays += [previous, following, first, second]
        pieces += [
            (which, y_size - 1, 0, half_z),
            (which, 1, 0, half_z),
            (which, 2, 0, half_z // 2),
            (which, 2, half_z // 2, half_z // 2),
        ]
    place = jnp.stack([lax.axis_index("z") % 2, lax.axis_index("y")]).astype(jnp.int32)
    partial_value = pl.pallas_call(
        functools.partial(
            aggregate_kernel, pieces=pieces, source_count=source_count, tile=tile
        ),
        out_shape=jax.ShapeDtypeStruct((target_count * tile, width), jnp.float32),
        in_specs=[pl.BlockSpec(memory_space=pltpu.SMEM)] * 3
        + [pl.BlockSpec(memory_space=pl.ANY)] * (1 + len(arrays)),
        out_specs=pl.BlockSpec(memory_space=pltpu.VMEM),
        scratch_shapes=[
            pltpu.VMEM((source_count, target_count * tile, tile), jnp.bfloat16),
            pltpu.VMEM((half_z, 2, y_size, rows, width), jnp.bfloat16),
            pltpu.SemaphoreType.DMA(()),
            pltpu.SemaphoreType.DMA((len(arrays),)),
        ],
        compiler_params=pltpu.CompilerParams(vmem_limit_bytes=32 * 1024 * 1024),
    )(place, tile_coord[0, 0], tile_count[0], adj_tiles[0, 0], *arrays)
    parts = lax.all_to_all(
        partial_value.reshape(row_size, rows, width), "row", 0, 0, tiled=True
    )
    hidden = jnp.sum(parts, axis=0).astype(jnp.bfloat16)
    mixed = jnp.dot(hidden, weight, preferred_element_type=jnp.float32)
    return jax.nn.relu(mixed).astype(jnp.bfloat16)


def solution(mesh):
    devices = mesh.devices
    split = Mesh(
        devices.reshape(devices.shape[0], devices.shape[1] // Y_RING, Y_RING),
        ("row", "z", "y"),
    )
    col = ("z", "y")
    return jax.shard_map(
        on_device,
        mesh=split,
        in_specs=(
            P(("row", "z", "y"), None),
            P("row", col, None, None, None),
            P("row", col, None),
            P("row", col),
            P(),
        ),
        out_specs=P(("z", "y", "row"), None),
        check_vma=False,
    )
```

```python
import functools

import jax
import jax.numpy as jnp
from jax import lax
from jax.experimental import pallas as pl
from jax.experimental.pallas import tpu as pltpu
from jax.sharding import Mesh, PartitionSpec as P

Y_RING = 4


def ring_shift(value, axis, step):
    size = lax.axis_size(axis)
    return lax.ppermute(value, axis, [(i, (i + step) % size) for i in range(size)])


def spread_kernel(
    coord_ref, count_ref, adj_ref, dense_ref, dense, tile_sem, out_sem, *, source_count, tile
):
    def clear(index, carry):
        dense[index] = jnp.zeros(dense.shape[1:], dense.dtype)
        return carry

    lax.fori_loop(0, source_count, clear, 0)
    live = count_ref[0]

    def place(slot, carry):
        target = coord_ref[slot] // source_count
        source = coord_ref[slot] % source_count
        rows = pl.ds(pl.multiple_of(target * tile, tile), tile)
        pltpu.make_async_copy(adj_ref.at[slot], dense.at[source, rows], tile_sem).start()
        return carry

    lax.fori_loop(0, live, place, 0)

    def arrived(slot, carry):
        pltpu.make_async_copy(adj_ref.at[0], dense.at[0, pl.ds(0, tile)], tile_sem).wait()
        return carry

    lax.fori_loop(0, live, arrived, 0)
    out = pltpu.make_async_copy(dense, dense_ref, out_sem)
    out.start()
    out.wait()


def spread(adj_tiles, coord, count, target_count, source_count):
    tile = adj_tiles.shape[-1]
    shape = (source_count, target_count * tile, tile)
    return pl.pallas_call(
        functools.partial(spread_kernel, source_count=source_count, tile=tile),
        out_shape=jax.ShapeDtypeStruct(shape, jnp.bfloat16),
        in_specs=[pl.BlockSpec(memory_space=pltpu.SMEM)] * 2
        + [pl.BlockSpec(memory_space=pltpu.HBM)],
        out_specs=pl.BlockSpec(memory_space=pltpu.HBM),
        scratch_shapes=[
            pltpu.VMEM(shape, jnp.bfloat16),
            pltpu.SemaphoreType.DMA(()),
            pltpu.SemaphoreType.DMA(()),
        ],
        cost_estimate=pl.CostEstimate(
            flops=0, bytes_accessed=12 * 1024 * 1024, transcendentals=0
        ),
    )(coord, count, adj_tiles)


def multiply_kernel(dense_ref, *refs, spots, across, added):
    base_ref = refs[0] if added else None
    piece_refs = refs[added : added + len(spots)]
    out_ref, feats, dense, feat_sems, dense_sems = refs[added + len(spots) :]
    half = (lax.axis_index("z") + across) % 2
    own_y = lax.axis_index("y")
    y_size, z_count, rows, width = feats.shape
    tile = dense.shape[-1]
    per_z = y_size * rows // tile
    copies = []
    for index, (ref, offset) in enumerate(zip(piece_refs, spots)):
        into = feats if offset is None else feats.at[(own_y + offset) % Y_RING]
        copies.append(pltpu.make_async_copy(ref, into, feat_sems.at[index]))
    columns = []
    for z in range(z_count):
        source = dense_ref.at[pl.ds((2 * z + half) * per_z, per_z)]
        columns.append(pltpu.make_async_copy(source, dense.at[z], dense_sems.at[z]))
    for copy in copies + columns:
        copy.start()
    for copy in copies:
        copy.wait()
    per_step = 4
    for at in range(0, z_count, per_step):
        left, right = [], []
        for z in range(at, at + per_step):
            columns[z].wait()
            left += [dense[z, k] for k in range(per_z)]
            right += [feats[k, z] for k in range(y_size)]
        product = jnp.dot(
            jnp.concatenate(left, axis=1),
            jnp.concatenate(right, axis=0),
            preferred_element_type=jnp.float32,
        )
        if at > 0:
            out_ref[...] += product
        elif added:
            out_ref[...] = base_ref[...] + product
        else:
            out_ref[...] = product


def multiply(dense, pieces, spots, across, y_size, base=None):
    z_count, rows, width = pieces[0].shape[-3:]
    tile = dense.shape[-1]
    per_z = y_size * rows // tile
    out = jax.ShapeDtypeStruct((dense.shape[1], width), jnp.float32)
    added = 0 if base is None else 1
    return pl.pallas_call(
        functools.partial(multiply_kernel, spots=spots, across=across, added=added),
        out_shape=out,
        in_specs=[pl.BlockSpec(memory_space=pltpu.HBM)]
        + [pl.BlockSpec(memory_space=pltpu.VMEM)] * added
        + [pl.BlockSpec(memory_space=pltpu.HBM)] * len(pieces),
        out_specs=pl.BlockSpec(memory_space=pltpu.VMEM),
        scratch_shapes=[
            pltpu.VMEM((y_size, z_count, rows, width), jnp.bfloat16),
            pltpu.VMEM((z_count, per_z, dense.shape[1], tile), jnp.bfloat16),
            pltpu.SemaphoreType.DMA((len(pieces),)),
            pltpu.SemaphoreType.DMA((z_count,)),
        ],
        cost_estimate=pl.CostEstimate(
            flops=2 * dense.shape[1] * z_count * y_size * rows * width,
            bytes_accessed=6 * 1024 * 1024,
            transcendentals=0,
        ),
    )(dense, *([base] if added else []), *pieces)


def on_device(features, adj_tiles, tile_coord, tile_count, weight):
    tile = adj_tiles.shape[-1]
    rows, width = features.shape
    z_size, y_size = lax.axis_size("z"), lax.axis_size("y")
    row_size = lax.axis_size("row")
    target_count = rows * row_size // tile
    source_count = rows * z_size * y_size // tile
    half_z = z_size // 2
    groups = [[i + 2 * j for j in range(half_z)] for i in range(2)]
    own = lax.all_gather(features, "z", axis=0, axis_index_groups=groups)
    own_all = lax.all_gather(own, "y", axis=0)
    quarter = half_z // 2
    other = jnp.concatenate(
        [ring_shift(own[:quarter], "z", 1), ring_shift(own[quarter:], "z", -1)], axis=0
    )
    previous = ring_shift(other, "y", 1)
    following = ring_shift(other, "y", -1)
    opposite = ring_shift(following, "y", -1)

    dense = spread(adj_tiles[0, 0], tile_coord[0, 0], tile_count[0], target_count, source_count)
    first = multiply(dense, [own_all], [None], 0, y_size)
    partial_value = multiply(
        dense,
        [other, previous, following, opposite],
        [0, y_size - 1, 1, 2],
        1,
        y_size,
        first,
    )
    parts = lax.all_to_all(
        partial_value.reshape(row_size, rows, width), "row", 0, 0, tiled=True
    )
    hidden = jnp.sum(parts, axis=0).astype(jnp.bfloat16)
    mixed = jnp.dot(hidden, weight, preferred_element_type=jnp.float32)
    return jax.nn.relu(mixed).astype(jnp.bfloat16)


def solution(mesh):
    devices = mesh.devices
    split = Mesh(
        devices.reshape(devices.shape[0], devices.shape[1] // Y_RING, Y_RING),
        ("row", "z", "y"),
    )
    col = ("z", "y")
    return jax.shard_map(
        on_device,
        mesh=split,
        in_specs=(
            P(("row", "z", "y"), None),
            P("row", col, None, None, None),
            P("row", col, None),
            P("row", col),
            P(),
        ),
        out_specs=P(("z", "y", "row"), None),
        check_vma=False,
    )
```

```python
import functools

import jax
import jax.numpy as jnp
from jax import lax
from jax.experimental import pallas as pl
from jax.experimental.pallas import tpu as pltpu
from jax.sharding import Mesh, PartitionSpec as P

Y_RING = 4
VMEM_GRANT = 24 * 1024 * 1024


def ring_shift(value, axis, step):
    size = lax.axis_size(axis)
    return lax.ppermute(value, axis, [(i, (i + step) % size) for i in range(size)])


def spread_kernel(coord_ref, count_ref, adj_ref, dense, sem, *, source_count, tile):
    def clear(index, carry):
        dense[index] = jnp.zeros(dense.shape[1:], dense.dtype)
        return carry

    lax.fori_loop(0, source_count, clear, 0)
    live = count_ref[0]

    def place(slot, carry):
        target = coord_ref[slot] // source_count
        source = coord_ref[slot] % source_count
        rows = pl.ds(pl.multiple_of(target * tile, tile), tile)
        pltpu.make_async_copy(adj_ref.at[slot], dense.at[source, rows], sem).start()
        return carry

    lax.fori_loop(0, live, place, 0)

    def arrived(slot, carry):
        pltpu.make_async_copy(adj_ref.at[0], dense.at[0, pl.ds(0, tile)], sem).wait()
        return carry

    lax.fori_loop(0, live, arrived, 0)


def spread(adj_tiles, coord, count, target_count, source_count):
    tile = adj_tiles.shape[-1]
    return pl.pallas_call(
        functools.partial(spread_kernel, source_count=source_count, tile=tile),
        out_shape=jax.ShapeDtypeStruct(
            (source_count, target_count * tile, tile), jnp.bfloat16
        ),
        in_specs=[pl.BlockSpec(memory_space=pltpu.SMEM)] * 2
        + [pl.BlockSpec(memory_space=pltpu.HBM)],
        out_specs=pl.BlockSpec(memory_space=pltpu.VMEM),
        scratch_shapes=[pltpu.SemaphoreType.DMA(())],
        compiler_params=pltpu.CompilerParams(vmem_limit_bytes=VMEM_GRANT),
        cost_estimate=pl.CostEstimate(
            flops=0, bytes_accessed=12 * 1024 * 1024, transcendentals=0
        ),
    )(coord, count, adj_tiles)


def multiply_kernel(dense, *refs, spots, across, added):
    base_ref = refs[0] if added else None
    piece_refs = refs[added : added + len(spots)]
    out_ref, feats = refs[added + len(spots) :]
    half = (lax.axis_index("z") + across) % 2
    own_y = lax.axis_index("y")
    y_size, z_count, rows, width = feats.shape
    tile = dense.shape[-1]
    per_z = y_size * rows // tile
    for ref, offset in zip(piece_refs, spots):
        feats[(own_y + offset) % y_size] = ref[...]
    per_step = 4
    for at in range(0, z_count, per_step):
        left, right = [], []
        for z in range(at, at + per_step):
            left += [dense[(2 * z + half) * per_z + k] for k in range(per_z)]
            right += [feats[k, z] for k in range(y_size)]
        product = jnp.dot(
            jnp.concatenate(left, axis=1),
            jnp.concatenate(right, axis=0),
            preferred_element_type=jnp.float32,
        )
        if at > 0:
            out_ref[...] += product
        elif added:
            out_ref[...] = base_ref[...] + product
        else:
            out_ref[...] = product


def multiply(dense, pieces, spots, across, base=None):
    z_count, rows, width = pieces[0].shape
    added = 0 if base is None else 1
    arrays = [dense] + ([base] if added else []) + pieces
    return pl.pallas_call(
        functools.partial(multiply_kernel, spots=spots, across=across, added=added),
        out_shape=jax.ShapeDtypeStruct((dense.shape[1], width), jnp.float32),
        in_specs=[pl.BlockSpec(memory_space=pltpu.VMEM)] * len(arrays),
        out_specs=pl.BlockSpec(memory_space=pltpu.VMEM),
        scratch_shapes=[pltpu.VMEM((len(spots), z_count, rows, width), jnp.bfloat16)],
        compiler_params=pltpu.CompilerParams(vmem_limit_bytes=VMEM_GRANT),
        cost_estimate=pl.CostEstimate(
            flops=2 * dense.shape[1] * z_count * len(spots) * rows * width,
            bytes_accessed=6 * 1024 * 1024,
            transcendentals=0,
        ),
    )(*arrays)


def on_device(features, adj_tiles, tile_coord, tile_count, weight):
    tile = adj_tiles.shape[-1]
    rows, width = features.shape
    z_size, y_size = lax.axis_size("z"), lax.axis_size("y")
    row_size = lax.axis_size("row")
    target_count = rows * row_size // tile
    source_count = rows * z_size * y_size // tile
    half_z = z_size // 2
    groups = [[i + 2 * j for j in range(half_z)] for i in range(2)]
    own = lax.all_gather(features, "z", axis=0, axis_index_groups=groups)
    spots = [2, 1, y_size - 1, 0]
    near = [ring_shift(own, "y", -spot) for spot in spots[:-1]] + [own]
    far = [ring_shift(piece, "z", (-1) ** at) for at, piece in enumerate(near)]

    dense = spread(adj_tiles[0, 0], tile_coord[0, 0], tile_count[0], target_count, source_count)
    first = multiply(dense, near, spots, 0)
    partial_value = multiply(dense, far, spots, 1, first)
    parts = lax.all_to_all(
        partial_value.reshape(row_size, rows, width), "row", 0, 0, tiled=True
    )
    hidden = jnp.sum(parts, axis=0).astype(jnp.bfloat16)
    mixed = jnp.dot(hidden, weight, preferred_element_type=jnp.float32)
    return jax.nn.relu(mixed).astype(jnp.bfloat16)


def solution(mesh):
    devices = mesh.devices
    split = Mesh(
        devices.reshape(devices.shape[0], devices.shape[1] // Y_RING, Y_RING),
        ("row", "z", "y"),
    )
    col = ("z", "y")
    return jax.shard_map(
        on_device,
        mesh=split,
        in_specs=(
            P(("row", "z", "y"), None),
            P("row", col, None, None, None),
            P("row", col, None),
            P("row", col),
            P(),
        ),
        out_specs=P(("z", "y", "row"), None),
        check_vma=False,
    )
```

```python
import functools

import jax
import jax.numpy as jnp
from jax import lax
from jax.experimental import pallas as pl
from jax.experimental.pallas import tpu as pltpu
from jax.sharding import Mesh, PartitionSpec as P

Y_RING = 4
VMEM_GRANT = 24 * 1024 * 1024


def ring_shift(value, axis, step):
    size = lax.axis_size(axis)
    return lax.ppermute(value, axis, [(i, (i + step) % size) for i in range(size)])


def spread_kernel(coord_ref, count_ref, adj_ref, dense, sem, *, source_count, tile):
    slots = adj_ref.shape[2]
    group = 8

    def clear(index, carry):
        dense[index] = jnp.zeros(dense.shape[1:], dense.dtype)
        return carry

    lax.fori_loop(0, source_count, clear, 0)
    live = count_ref[0, 0]

    def place(slot):
        spot = coord_ref[0, 0, slot]
        target = lax.div(spot, source_count)
        source = lax.rem(spot, source_count)
        rows = pl.ds(pl.multiple_of(target * tile, tile), tile)
        pltpu.make_async_copy(adj_ref.at[0, 0, slot], dense.at[source, rows], sem).start()

    def place_group(at, carry):
        for i in range(group):
            place(at * group + i)
        return carry

    def place_one(slot, carry):
        place(slot)
        return carry

    whole = lax.div(live, group)
    lax.fori_loop(0, whole, place_group, 0)
    lax.fori_loop(whole * group, live, place_one, 0)
    amount = 1
    while amount <= slots:

        @pl.when(lax.rem(lax.div(live, amount), 2) == 1)
        def arrived():
            some = adj_ref.at[0, 0, pl.ds(0, amount)]
            pltpu.make_async_copy(some, some, sem).wait()

        amount *= 2


def spread(adj_tiles, coord, count, target_count, source_count):
    tile = adj_tiles.shape[-1]
    shape = (source_count, target_count * tile, tile)
    return pl.pallas_call(
        functools.partial(spread_kernel, source_count=source_count, tile=tile),
        out_shape=jax.ShapeDtypeStruct(shape, jnp.bfloat16),
        in_specs=[pl.BlockSpec(memory_space=pltpu.SMEM)] * 2
        + [pl.BlockSpec(memory_space=pltpu.HBM)],
        out_specs=pl.BlockSpec(memory_space=pltpu.VMEM),
        scratch_shapes=[pltpu.SemaphoreType.DMA(())],
        compiler_params=pltpu.CompilerParams(vmem_limit_bytes=VMEM_GRANT),
        cost_estimate=pl.CostEstimate(
            flops=0, bytes_accessed=12 * 1024 * 1024, transcendentals=0
        ),
    )(
        pltpu.with_memory_space_constraint(coord, pltpu.HBM),
        count,
        pltpu.with_memory_space_constraint(adj_tiles, pltpu.HBM),
    )


def multiply_kernel(dense, *refs, spots, across, added):
    base_ref = refs[0] if added else None
    piece_refs = refs[added : added + len(spots)]
    out_ref, feats = refs[added + len(spots) :]
    half = (lax.axis_index("z") + across) % 2
    own_y = lax.axis_index("y")
    y_size, z_count, rows, width = feats.shape
    tile = dense.shape[-1]
    per_z = y_size * rows // tile
    for ref, offset in zip(piece_refs, spots):
        feats[(own_y + offset) % y_size] = ref[...]
    per_step = 4
    for at in range(0, z_count, per_step):
        left, right = [], []
        for z in range(at, at + per_step):
            left += [dense[(2 * z + half) * per_z + k] for k in range(per_z)]
            right += [feats[k, z] for k in range(y_size)]
        product = jnp.dot(
            jnp.concatenate(left, axis=1),
            jnp.concatenate(right, axis=0),
            preferred_element_type=jnp.float32,
        )
        if at > 0:
            out_ref[...] += product
        elif added:
            out_ref[...] = base_ref[...] + product
        else:
            out_ref[...] = product


def multiply(dense, pieces, spots, across, base=None):
    z_count, rows, width = pieces[0].shape
    added = 0 if base is None else 1
    arrays = [dense] + ([base] if added else []) + pieces
    return pl.pallas_call(
        functools.partial(multiply_kernel, spots=spots, across=across, added=added),
        out_shape=jax.ShapeDtypeStruct((dense.shape[1], width), jnp.float32),
        in_specs=[pl.BlockSpec(memory_space=pltpu.VMEM)] * len(arrays),
        out_specs=pl.BlockSpec(memory_space=pltpu.VMEM),
        scratch_shapes=[pltpu.VMEM((len(spots), z_count, rows, width), jnp.bfloat16)],
        compiler_params=pltpu.CompilerParams(vmem_limit_bytes=VMEM_GRANT),
        cost_estimate=pl.CostEstimate(
            flops=2 * dense.shape[1] * z_count * len(spots) * rows * width,
            bytes_accessed=6 * 1024 * 1024,
            transcendentals=0,
        ),
    )(*arrays)


def on_device(features, adj_tiles, tile_coord, tile_count, weight):
    tile = adj_tiles.shape[-1]
    rows, width = features.shape
    z_size, y_size = lax.axis_size("z"), lax.axis_size("y")
    row_size = lax.axis_size("row")
    target_count = rows * row_size // tile
    source_count = rows * z_size * y_size // tile
    half_z = z_size // 2
    groups = [[i + 2 * j for j in range(half_z)] for i in range(2)]
    own = lax.all_gather(features, "z", axis=0, axis_index_groups=groups)
    spots = [2, 1, y_size - 1, 0]
    near = [ring_shift(own, "y", -spot) for spot in spots[:-1]] + [own]
    far = [ring_shift(piece, "z", (-1) ** at) for at, piece in enumerate(near)]

    dense = spread(adj_tiles, tile_coord, tile_count, target_count, source_count)
    first = multiply(dense, near, spots, 0)
    partial_value = multiply(dense, far, spots, 1, first)
    parts = lax.all_to_all(
        partial_value.reshape(row_size, rows, width), "row", 0, 0, tiled=True
    )
    hidden = jnp.sum(parts, axis=0).astype(jnp.bfloat16)
    mixed = jnp.dot(hidden, weight, preferred_element_type=jnp.float32)
    return jax.nn.relu(mixed).astype(jnp.bfloat16)


def solution(mesh):
    devices = mesh.devices
    split = Mesh(
        devices.reshape(devices.shape[0], devices.shape[1] // Y_RING, Y_RING),
        ("row", "z", "y"),
    )
    col = ("z", "y")
    return jax.shard_map(
        on_device,
        mesh=split,
        in_specs=(
            P(("row", "z", "y"), None),
            P("row", col, None, None, None),
            P("row", col, None),
            P("row", col),
            P(),
        ),
        out_specs=P(("z", "y", "row"), None),
        check_vma=False,
    )
```

```python
import functools

import jax
import jax.numpy as jnp
from jax import lax
from jax.experimental import pallas as pl
from jax.experimental.pallas import tpu as pltpu
from jax.sharding import Mesh, PartitionSpec as P

Y_RING = 4
VMEM_GRANT = 24 * 1024 * 1024


def ring_shift(value, axis, step):
    size = lax.axis_size(axis)
    return lax.ppermute(value, axis, [(i, (i + step) % size) for i in range(size)])


def spread_kernel(coord_ref, count_ref, adj_ref, dense, sem, *, source_count, tile):
    slots = adj_ref.shape[2]
    group = 8

    def clear(index, carry):
        dense[index] = jnp.zeros(dense.shape[1:], dense.dtype)
        return carry

    lax.fori_loop(0, source_count, clear, 0)
    live = count_ref[0, 0]

    def place(slot):
        spot = coord_ref[0, 0, slot]
        target = lax.div(spot, source_count)
        source = lax.rem(spot, source_count)
        rows = pl.ds(pl.multiple_of(target * tile, tile), tile)
        pltpu.make_async_copy(adj_ref.at[0, 0, slot], dense.at[source, rows], sem).start()

    def place_group(at, carry):
        for i in range(group):
            place(at * group + i)
        return carry

    def place_one(slot, carry):
        place(slot)
        return carry

    whole = lax.div(live, group)
    lax.fori_loop(0, whole, place_group, 0)
    lax.fori_loop(whole * group, live, place_one, 0)
    amount = 1
    while amount <= slots:

        @pl.when(lax.rem(lax.div(live, amount), 2) == 1)
        def arrived():
            some = adj_ref.at[0, 0, pl.ds(0, amount)]
            pltpu.make_async_copy(some, some, sem).wait()

        amount *= 2


def spread(adj_tiles, coord, count, target_count, source_count):
    tile = adj_tiles.shape[-1]
    shape = (source_count, target_count * tile, tile)
    return pl.pallas_call(
        functools.partial(spread_kernel, source_count=source_count, tile=tile),
        out_shape=jax.ShapeDtypeStruct(shape, jnp.bfloat16),
        in_specs=[pl.BlockSpec(memory_space=pltpu.SMEM)] * 2
        + [pl.BlockSpec(memory_space=pltpu.HBM)],
        out_specs=pl.BlockSpec(memory_space=pltpu.VMEM),
        scratch_shapes=[pltpu.SemaphoreType.DMA(())],
        compiler_params=pltpu.CompilerParams(vmem_limit_bytes=VMEM_GRANT),
        cost_estimate=pl.CostEstimate(
            flops=0, bytes_accessed=12 * 1024 * 1024, transcendentals=0
        ),
    )(
        pltpu.with_memory_space_constraint(coord, pltpu.HBM),
        count,
        pltpu.with_memory_space_constraint(adj_tiles, pltpu.HBM),
    )


def multiply_kernel(dense, *refs, spots, across, added):
    base_ref = refs[0] if added else None
    piece_refs = refs[added : added + len(spots)]
    out_ref, feats = refs[added + len(spots) :]
    half = (lax.axis_index("z") + across) % 2
    own_y = lax.axis_index("y")
    y_size, z_count, rows, width = feats.shape
    tile = dense.shape[-1]
    per_z = y_size * rows // tile
    for ref, offset in zip(piece_refs, spots):
        feats[(own_y + offset) % y_size] = ref[...]
    per_step = 4
    for at in range(0, z_count, per_step):
        left, right = [], []
        for z in range(at, at + per_step):
            left += [dense[(2 * z + half) * per_z + k] for k in range(per_z)]
            right += [feats[k, z] for k in range(y_size)]
        product = jnp.dot(
            jnp.concatenate(left, axis=1),
            jnp.concatenate(right, axis=0),
            preferred_element_type=jnp.float32,
        )
        if at > 0:
            out_ref[...] += product
        elif added:
            out_ref[...] = base_ref[...] + product
        else:
            out_ref[...] = product


def multiply(dense, pieces, spots, across, base=None):
    z_count, rows, width = pieces[0].shape
    added = 0 if base is None else 1
    arrays = [dense] + ([base] if added else []) + pieces
    return pl.pallas_call(
        functools.partial(multiply_kernel, spots=spots, across=across, added=added),
        out_shape=jax.ShapeDtypeStruct((dense.shape[1], width), jnp.float32),
        in_specs=[pl.BlockSpec(memory_space=pltpu.VMEM)] * len(arrays),
        out_specs=pl.BlockSpec(memory_space=pltpu.VMEM),
        scratch_shapes=[pltpu.VMEM((len(spots), z_count, rows, width), jnp.bfloat16)],
        compiler_params=pltpu.CompilerParams(vmem_limit_bytes=VMEM_GRANT),
        cost_estimate=pl.CostEstimate(
            flops=2 * dense.shape[1] * z_count * len(spots) * rows * width,
            bytes_accessed=6 * 1024 * 1024,
            transcendentals=0,
        ),
    )(*arrays)


def on_device(features, adj_tiles, tile_coord, tile_count, weight):
    tile = adj_tiles.shape[-1]
    rows, width = features.shape
    z_size, y_size = lax.axis_size("z"), lax.axis_size("y")
    row_size = lax.axis_size("row")
    target_count = rows * row_size // tile
    source_count = rows * z_size * y_size // tile
    half_z = z_size // 2
    groups = [[i + 2 * j for j in range(half_z)] for i in range(2)]
    own = lax.all_gather(features, "z", axis=0, axis_index_groups=groups)
    spots = [1, y_size - 1, 2, 0]
    near = [ring_shift(own, "y", -spot) for spot in spots[:-1]] + [own]
    far = [ring_shift(piece, "z", (-1) ** at) for at, piece in enumerate(near)]

    dense = spread(adj_tiles, tile_coord, tile_count, target_count, source_count)
    first = multiply(dense, near, spots, 0)
    partial_value = multiply(dense, far, spots, 1, first)
    parts = lax.all_to_all(
        partial_value.reshape(row_size, rows, width), "row", 0, 0, tiled=True
    )
    hidden = jnp.sum(parts, axis=0).astype(jnp.bfloat16)
    mixed = jnp.dot(hidden, weight, preferred_element_type=jnp.float32)
    return jax.nn.relu(mixed).astype(jnp.bfloat16)


def solution(mesh):
    devices = mesh.devices
    split = Mesh(
        devices.reshape(devices.shape[0], devices.shape[1] // Y_RING, Y_RING),
        ("row", "z", "y"),
    )
    col = ("z", "y")
    return jax.shard_map(
        on_device,
        mesh=split,
        in_specs=(
            P(("row", "z", "y"), None),
            P("row", col, None, None, None),
            P("row", col, None),
            P("row", col),
            P(),
        ),
        out_specs=P(("z", "y", "row"), None),
        check_vma=False,
    )
```

```python
import functools

import jax
import jax.numpy as jnp
from jax import lax
from jax.experimental import pallas as pl
from jax.experimental.pallas import tpu as pltpu
from jax.sharding import Mesh, PartitionSpec as P

Y_RING = 4
VMEM_GRANT = 24 * 1024 * 1024


def ring_shift(value, axis, step):
    size = lax.axis_size(axis)
    return lax.ppermute(value, axis, [(i, (i + step) % size) for i in range(size)])


def spread_kernel(coord_ref, count_ref, adj_ref, dense, sem, *, source_count, tile):
    slots = adj_ref.shape[2]
    group = 8

    def clear(index, carry):
        dense[index] = jnp.zeros(dense.shape[1:], dense.dtype)
        return carry

    lax.fori_loop(0, source_count, clear, 0)
    live = count_ref[0, 0]

    def place(slot):
        spot = coord_ref[0, 0, slot]
        target = lax.div(spot, source_count)
        source = lax.rem(spot, source_count)
        rows = pl.ds(pl.multiple_of(target * tile, tile), tile)
        pltpu.make_async_copy(adj_ref.at[0, 0, slot], dense.at[source, rows], sem).start()

    def place_group(at, carry):
        for i in range(group):
            place(at * group + i)
        return carry

    def place_one(slot, carry):
        place(slot)
        return carry

    whole = lax.div(live, group)
    lax.fori_loop(0, whole, place_group, 0)
    lax.fori_loop(whole * group, live, place_one, 0)
    amount = 1
    while amount <= slots:

        @pl.when(lax.rem(lax.div(live, amount), 2) == 1)
        def arrived():
            some = adj_ref.at[0, 0, pl.ds(0, amount)]
            pltpu.make_async_copy(some, some, sem).wait()

        amount *= 2


def spread(adj_tiles, coord, count, target_count, source_count):
    tile = adj_tiles.shape[-1]
    shape = (source_count, target_count * tile, tile)
    return pl.pallas_call(
        functools.partial(spread_kernel, source_count=source_count, tile=tile),
        out_shape=jax.ShapeDtypeStruct(shape, jnp.bfloat16),
        in_specs=[pl.BlockSpec(memory_space=pltpu.SMEM)] * 2
        + [pl.BlockSpec(memory_space=pltpu.HBM)],
        out_specs=pl.BlockSpec(memory_space=pltpu.VMEM),
        scratch_shapes=[pltpu.SemaphoreType.DMA(())],
        compiler_params=pltpu.CompilerParams(vmem_limit_bytes=VMEM_GRANT),
        cost_estimate=pl.CostEstimate(
            flops=0, bytes_accessed=12 * 1024 * 1024, transcendentals=0
        ),
    )(
        pltpu.with_memory_space_constraint(coord, pltpu.HBM),
        count,
        pltpu.with_memory_space_constraint(adj_tiles, pltpu.HBM),
    )


def multiply_kernel(dense, *refs, spots, across, added):
    base_ref = refs[0] if added else None
    piece_refs = refs[added : added + len(spots)]
    out_ref, feats, total = refs[added + len(spots) :]
    half = (lax.axis_index("z") + across) % 2
    own_y = lax.axis_index("y")
    y_size, z_count, rows, width = feats.shape
    tile = dense.shape[-1]
    per_z = y_size * rows // tile
    for ref, offset in zip(piece_refs, spots):
        feats[(own_y + offset) % y_size] = ref[...]
    per_step = 4
    for at in range(0, z_count, per_step):
        left, right = [], []
        for z in range(at, at + per_step):
            left += [dense[(2 * z + half) * per_z + k] for k in range(per_z)]
            right += [feats[k, z] for k in range(y_size)]
        product = jnp.dot(
            jnp.concatenate(left, axis=1),
            jnp.concatenate(right, axis=0),
            preferred_element_type=jnp.float32,
        )
        if at > 0:
            product += total[...]
        elif added:
            product += base_ref[...]
        if at + per_step < z_count:
            total[...] = product
        else:
            out_ref[...] = product.astype(out_ref.dtype)


def multiply(dense, pieces, spots, across, kind, base=None):
    z_count, rows, width = pieces[0].shape
    added = 0 if base is None else 1
    arrays = [dense] + ([base] if added else []) + pieces
    shape = (dense.shape[1], width)
    return pl.pallas_call(
        functools.partial(multiply_kernel, spots=spots, across=across, added=added),
        out_shape=jax.ShapeDtypeStruct(shape, kind),
        in_specs=[pl.BlockSpec(memory_space=pltpu.VMEM)] * len(arrays),
        out_specs=pl.BlockSpec(memory_space=pltpu.VMEM),
        scratch_shapes=[
            pltpu.VMEM((len(spots), z_count, rows, width), jnp.bfloat16),
            pltpu.VMEM(shape, jnp.float32),
        ],
        compiler_params=pltpu.CompilerParams(vmem_limit_bytes=VMEM_GRANT),
        cost_estimate=pl.CostEstimate(
            flops=2 * dense.shape[1] * z_count * len(spots) * rows * width,
            bytes_accessed=6 * 1024 * 1024,
            transcendentals=0,
        ),
    )(*arrays)


def on_device(features, adj_tiles, tile_coord, tile_count, weight):
    tile = adj_tiles.shape[-1]
    rows, width = features.shape
    z_size, y_size = lax.axis_size("z"), lax.axis_size("y")
    row_size = lax.axis_size("row")
    target_count = rows * row_size // tile
    source_count = rows * z_size * y_size // tile
    half_z = z_size // 2
    groups = [[i + 2 * j for j in range(half_z)] for i in range(2)]
    own = lax.all_gather(features, "z", axis=0, axis_index_groups=groups)
    spots = [2, 1, y_size - 1, 0]
    near = [ring_shift(own, "y", -spot) for spot in spots[:-1]] + [own]
    far = [ring_shift(piece, "z", (-1) ** at) for at, piece in enumerate(near)]

    dense = spread(adj_tiles, tile_coord, tile_count, target_count, source_count)
    first = multiply(dense, near, spots, 0, jnp.float32)
    partial_value = multiply(dense, far, spots, 1, jnp.bfloat16, first)
    parts = lax.all_to_all(
        partial_value.reshape(row_size, rows, width), "row", 0, 0, tiled=True
    )
    hidden = jnp.sum(parts.astype(jnp.float32), axis=0).astype(jnp.bfloat16)
    mixed = jnp.dot(hidden, weight, preferred_element_type=jnp.float32)
    return jax.nn.relu(mixed).astype(jnp.bfloat16)


def solution(mesh):
    devices = mesh.devices
    split = Mesh(
        devices.reshape(devices.shape[0], devices.shape[1] // Y_RING, Y_RING),
        ("row", "z", "y"),
    )
    col = ("z", "y")
    return jax.shard_map(
        on_device,
        mesh=split,
        in_specs=(
            P(("row", "z", "y"), None),
            P("row", col, None, None, None),
            P("row", col, None),
            P("row", col),
            P(),
        ),
        out_specs=P(("z", "y", "row"), None),
        check_vma=False,
    )
```

```python
import functools

import jax
import jax.numpy as jnp
from jax import lax
from jax.experimental import pallas as pl
from jax.experimental.pallas import tpu as pltpu
from jax.sharding import Mesh, PartitionSpec as P

Y_RING = 4
VMEM_GRANT = 24 * 1024 * 1024
SENT_SCALE = 16.0


def ring_shift(value, axis, step):
    size = lax.axis_size(axis)
    return lax.ppermute(value, axis, [(i, (i + step) % size) for i in range(size)])


def spread_kernel(coord_ref, count_ref, adj_ref, dense, sem, *, source_count, tile):
    slots = adj_ref.shape[2]
    group = 8

    def clear(index, carry):
        dense[index] = jnp.zeros(dense.shape[1:], dense.dtype)
        return carry

    lax.fori_loop(0, source_count, clear, 0)
    live = count_ref[0, 0]

    def place(slot):
        spot = coord_ref[0, 0, slot]
        target = lax.div(spot, source_count)
        source = lax.rem(spot, source_count)
        rows = pl.ds(pl.multiple_of(target * tile, tile), tile)
        pltpu.make_async_copy(adj_ref.at[0, 0, slot], dense.at[source, rows], sem).start()

    def place_group(at, carry):
        for i in range(group):
            place(at * group + i)
        return carry

    def place_one(slot, carry):
        place(slot)
        return carry

    whole = lax.div(live, group)
    lax.fori_loop(0, whole, place_group, 0)
    lax.fori_loop(whole * group, live, place_one, 0)
    amount = 1
    while amount <= slots:

        @pl.when(lax.rem(lax.div(live, amount), 2) == 1)
        def arrived():
            some = adj_ref.at[0, 0, pl.ds(0, amount)]
            pltpu.make_async_copy(some, some, sem).wait()

        amount *= 2


def spread(adj_tiles, coord, count, target_count, source_count):
    tile = adj_tiles.shape[-1]
    shape = (source_count, target_count * tile, tile)
    return pl.pallas_call(
        functools.partial(spread_kernel, source_count=source_count, tile=tile),
        out_shape=jax.ShapeDtypeStruct(shape, jnp.bfloat16),
        in_specs=[pl.BlockSpec(memory_space=pltpu.SMEM)] * 2
        + [pl.BlockSpec(memory_space=pltpu.HBM)],
        out_specs=pl.BlockSpec(memory_space=pltpu.VMEM),
        scratch_shapes=[pltpu.SemaphoreType.DMA(())],
        compiler_params=pltpu.CompilerParams(vmem_limit_bytes=VMEM_GRANT),
        cost_estimate=pl.CostEstimate(
            flops=0, bytes_accessed=12 * 1024 * 1024, transcendentals=0
        ),
    )(
        pltpu.with_memory_space_constraint(coord, pltpu.HBM),
        count,
        pltpu.with_memory_space_constraint(adj_tiles, pltpu.HBM),
    )


def multiply_kernel(dense, *refs, spots, across, scale, added):
    base_ref = refs[0] if added else None
    piece_refs = refs[added : added + len(spots)]
    out_ref, feats, total = refs[added + len(spots) :]
    half = (lax.axis_index("z") + across) % 2
    own_y = lax.axis_index("y")
    y_size, z_count, rows, width = feats.shape
    tile = dense.shape[-1]
    per_z = y_size * rows // tile
    for ref, offset in zip(piece_refs, spots):
        feats[(own_y + offset) % y_size] = ref[...]
    per_step = 4
    for at in range(0, z_count, per_step):
        left, right = [], []
        for z in range(at, at + per_step):
            left += [dense[(2 * z + half) * per_z + k] for k in range(per_z)]
            right += [feats[k, z] for k in range(y_size)]
        product = jnp.dot(
            jnp.concatenate(left, axis=1),
            jnp.concatenate(right, axis=0),
            preferred_element_type=jnp.float32,
        )
        if at > 0:
            product += total[...]
        elif added:
            product += base_ref[...]
        if at + per_step < z_count:
            total[...] = product
        else:
            out_ref[...] = (product * scale).astype(out_ref.dtype)


def multiply(dense, pieces, spots, across, kind, scale=1.0, base=None):
    z_count, rows, width = pieces[0].shape
    added = 0 if base is None else 1
    arrays = [dense] + ([base] if added else []) + pieces
    shape = (dense.shape[1], width)
    return pl.pallas_call(
        functools.partial(
            multiply_kernel, spots=spots, across=across, scale=scale, added=added
        ),
        out_shape=jax.ShapeDtypeStruct(shape, kind),
        in_specs=[pl.BlockSpec(memory_space=pltpu.VMEM)] * len(arrays),
        out_specs=pl.BlockSpec(memory_space=pltpu.VMEM),
        scratch_shapes=[
            pltpu.VMEM((len(spots), z_count, rows, width), jnp.bfloat16),
            pltpu.VMEM(shape, jnp.float32),
        ],
        compiler_params=pltpu.CompilerParams(vmem_limit_bytes=VMEM_GRANT),
        cost_estimate=pl.CostEstimate(
            flops=2 * dense.shape[1] * z_count * len(spots) * rows * width,
            bytes_accessed=6 * 1024 * 1024,
            transcendentals=0,
        ),
    )(*arrays)


def on_device(features, adj_tiles, tile_coord, tile_count, weight):
    tile = adj_tiles.shape[-1]
    rows, width = features.shape
    z_size, y_size = lax.axis_size("z"), lax.axis_size("y")
    row_size = lax.axis_size("row")
    target_count = rows * row_size // tile
    source_count = rows * z_size * y_size // tile
    half_z = z_size // 2
    groups = [[i + 2 * j for j in range(half_z)] for i in range(2)]
    own = lax.all_gather(features, "z", axis=0, axis_index_groups=groups)
    spots = [2, 1, y_size - 1, 0]
    near = [ring_shift(own, "y", -spot) for spot in spots[:-1]] + [own]
    far = [ring_shift(piece, "z", (-1) ** at) for at, piece in enumerate(near)]

    dense = spread(adj_tiles, tile_coord, tile_count, target_count, source_count)
    first = multiply(dense, near, spots, 0, jnp.float32)
    partial_value = multiply(dense, far, spots, 1, jnp.float32, SENT_SCALE, first)
    parts = lax.all_to_all(
        partial_value.astype(jnp.float16).reshape(row_size, rows, width), "row", 0, 0, tiled=True
    )
    hidden = jnp.sum(parts.astype(jnp.float32), axis=0) / SENT_SCALE
    hidden = hidden.astype(jnp.bfloat16)
    mixed = jnp.dot(hidden, weight, preferred_element_type=jnp.float32)
    return jax.nn.relu(mixed).astype(jnp.bfloat16)


def solution(mesh):
    devices = mesh.devices
    split = Mesh(
        devices.reshape(devices.shape[0], devices.shape[1] // Y_RING, Y_RING),
        ("row", "z", "y"),
    )
    col = ("z", "y")
    return jax.shard_map(
        on_device,
        mesh=split,
        in_specs=(
            P(("row", "z", "y"), None),
            P("row", col, None, None, None),
            P("row", col, None),
            P("row", col),
            P(),
        ),
        out_specs=P(("z", "y", "row"), None),
        check_vma=False,
    )
```

```python
import functools

import jax
import jax.numpy as jnp
from jax import lax
from jax.experimental import pallas as pl
from jax.experimental.pallas import tpu as pltpu
from jax.sharding import Mesh, PartitionSpec as P

Y_RING = 4
VMEM_GRANT = 24 * 1024 * 1024
SENT_SCALE = 16.0


def ring_shift(value, axis, step):
    rows, size = lax.axis_size("row"), lax.axis_size(axis)
    pairs = [
        (row * size + i, row * size + (i + (-1) ** row * step) % size)
        for row in range(rows)
        for i in range(size)
    ]
    return lax.ppermute(value, ("row", axis), pairs)


def spread_kernel(coord_ref, count_ref, adj_ref, dense, sem, *, source_count, tile):
    slots = adj_ref.shape[2]
    group = 8

    def clear(index, carry):
        dense[index] = jnp.zeros(dense.shape[1:], dense.dtype)
        return carry

    lax.fori_loop(0, source_count, clear, 0)
    live = count_ref[0, 0]

    def place(slot):
        spot = coord_ref[0, 0, slot]
        target = lax.div(spot, source_count)
        source = lax.rem(spot, source_count)
        rows = pl.ds(pl.multiple_of(target * tile, tile), tile)
        pltpu.make_async_copy(adj_ref.at[0, 0, slot], dense.at[source, rows], sem).start()

    def place_group(at, carry):
        for i in range(group):
            place(at * group + i)
        return carry

    def place_one(slot, carry):
        place(slot)
        return carry

    whole = lax.div(live, group)
    lax.fori_loop(0, whole, place_group, 0)
    lax.fori_loop(whole * group, live, place_one, 0)
    amount = 1
    while amount <= slots:

        @pl.when(lax.rem(lax.div(live, amount), 2) == 1)
        def arrived():
            some = adj_ref.at[0, 0, pl.ds(0, amount)]
            pltpu.make_async_copy(some, some, sem).wait()

        amount *= 2


def spread(adj_tiles, coord, count, target_count, source_count):
    tile = adj_tiles.shape[-1]
    shape = (source_count, target_count * tile, tile)
    return pl.pallas_call(
        functools.partial(spread_kernel, source_count=source_count, tile=tile),
        out_shape=jax.ShapeDtypeStruct(shape, jnp.bfloat16),
        in_specs=[pl.BlockSpec(memory_space=pltpu.SMEM)] * 2
        + [pl.BlockSpec(memory_space=pltpu.HBM)],
        out_specs=pl.BlockSpec(memory_space=pltpu.VMEM),
        scratch_shapes=[pltpu.SemaphoreType.DMA(())],
        compiler_params=pltpu.CompilerParams(vmem_limit_bytes=VMEM_GRANT),
        cost_estimate=pl.CostEstimate(
            flops=0, bytes_accessed=12 * 1024 * 1024, transcendentals=0
        ),
    )(
        pltpu.with_memory_space_constraint(coord, pltpu.HBM),
        count,
        pltpu.with_memory_space_constraint(adj_tiles, pltpu.HBM),
    )


def multiply_kernel(dense, *refs, spots, across, scale, added):
    base_ref = refs[0] if added else None
    piece_refs = refs[added : added + len(spots)]
    out_ref, feats, total = refs[added + len(spots) :]
    half = (lax.axis_index("z") + across) % 2
    own_y = lax.axis_index("y")
    turn = 1 - 2 * (lax.axis_index("row") % 2)
    y_size, z_count, rows, width = feats.shape
    tile = dense.shape[-1]
    per_z = y_size * rows // tile
    for ref, offset in zip(piece_refs, spots):
        feats[(own_y + turn * offset + y_size) % y_size] = ref[...]
    per_step = 4
    for at in range(0, z_count, per_step):
        left, right = [], []
        for z in range(at, at + per_step):
            left += [dense[(2 * z + half) * per_z + k] for k in range(per_z)]
            right += [feats[k, z] for k in range(y_size)]
        product = jnp.dot(
            jnp.concatenate(left, axis=1),
            jnp.concatenate(right, axis=0),
            preferred_element_type=jnp.float32,
        )
        if at > 0:
            product += total[...]
        elif added:
            product += base_ref[...]
        if at + per_step < z_count:
            total[...] = product
        else:
            out_ref[...] = (product * scale).astype(out_ref.dtype)


def multiply(dense, pieces, spots, across, kind, scale=1.0, base=None):
    z_count, rows, width = pieces[0].shape
    added = 0 if base is None else 1
    arrays = [dense] + ([base] if added else []) + pieces
    shape = (dense.shape[1], width)
    return pl.pallas_call(
        functools.partial(
            multiply_kernel, spots=spots, across=across, scale=scale, added=added
        ),
        out_shape=jax.ShapeDtypeStruct(shape, kind),
        in_specs=[pl.BlockSpec(memory_space=pltpu.VMEM)] * len(arrays),
        out_specs=pl.BlockSpec(memory_space=pltpu.VMEM),
        scratch_shapes=[
            pltpu.VMEM((len(spots), z_count, rows, width), jnp.bfloat16),
            pltpu.VMEM(shape, jnp.float32),
        ],
        compiler_params=pltpu.CompilerParams(vmem_limit_bytes=VMEM_GRANT),
        cost_estimate=pl.CostEstimate(
            flops=2 * dense.shape[1] * z_count * len(spots) * rows * width,
            bytes_accessed=6 * 1024 * 1024,
            transcendentals=0,
        ),
    )(*arrays)


def on_device(features, adj_tiles, tile_coord, tile_count, weight):
    tile = adj_tiles.shape[-1]
    rows, width = features.shape
    z_size, y_size = lax.axis_size("z"), lax.axis_size("y")
    row_size = lax.axis_size("row")
    target_count = rows * row_size // tile
    source_count = rows * z_size * y_size // tile
    half_z = z_size // 2
    groups = [[i + 2 * j for j in range(half_z)] for i in range(2)]
    own = lax.all_gather(features, "z", axis=0, axis_index_groups=groups)
    spots = [2, 1, y_size - 1, 0]
    near = [ring_shift(own, "y", -spot) for spot in spots[:-1]] + [own]
    far = [ring_shift(piece, "z", (-1) ** at) for at, piece in enumerate(near)]

    dense = spread(adj_tiles, tile_coord, tile_count, target_count, source_count)
    first = multiply(dense, near, spots, 0, jnp.float32)
    partial_value = multiply(dense, far, spots, 1, jnp.float32, SENT_SCALE, first)
    parts = lax.all_to_all(
        partial_value.astype(jnp.float16).reshape(row_size, rows, width), "row", 0, 0, tiled=True
    )
    hidden = jnp.sum(parts.astype(jnp.float32), axis=0) / SENT_SCALE
    hidden = hidden.astype(jnp.bfloat16)
    mixed = jnp.dot(hidden, weight, preferred_element_type=jnp.float32)
    return jax.nn.relu(mixed).astype(jnp.bfloat16)


def solution(mesh):
    devices = mesh.devices
    split = Mesh(
        devices.reshape(devices.shape[0], devices.shape[1] // Y_RING, Y_RING),
        ("row", "z", "y"),
    )
    col = ("z", "y")
    return jax.shard_map(
        on_device,
        mesh=split,
        in_specs=(
            P(("row", "z", "y"), None),
            P("row", col, None, None, None),
            P("row", col, None),
            P("row", col),
            P(),
        ),
        out_specs=P(("z", "y", "row"), None),
        check_vma=False,
    )
```

```python
import functools

import jax
import jax.numpy as jnp
from jax import lax
from jax.experimental import pallas as pl
from jax.experimental.pallas import tpu as pltpu
from jax.sharding import Mesh, PartitionSpec as P

Y_RING = 4
VMEM_GRANT = 24 * 1024 * 1024
SENT_SCALE = 16.0


def ring_shift(value, axis, step):
    rows, size = lax.axis_size("row"), lax.axis_size(axis)
    pairs = [
        (row * size + i, row * size + (i + (-1) ** row * step) % size)
        for row in range(rows)
        for i in range(size)
    ]
    return lax.ppermute(value, ("row", axis), pairs)


def spread_kernel(coord_ref, count_ref, adj_ref, dense, sem, *, source_count, tile):
    slots = adj_ref.shape[2]
    group = 8

    def clear(index, carry):
        dense[index] = jnp.zeros(dense.shape[1:], dense.dtype)
        return carry

    lax.fori_loop(0, source_count, clear, 0)
    live = count_ref[0, 0]

    def place(slot):
        spot = coord_ref[0, 0, slot]
        target = lax.div(spot, source_count)
        source = lax.rem(spot, source_count)
        rows = pl.ds(pl.multiple_of(target * tile, tile), tile)
        pltpu.make_async_copy(adj_ref.at[0, 0, slot], dense.at[source, rows], sem).start()

    def place_group(at, carry):
        for i in range(group):
            place(at * group + i)
        return carry

    def place_one(slot, carry):
        place(slot)
        return carry

    whole = lax.div(live, group)
    lax.fori_loop(0, whole, place_group, 0)
    lax.fori_loop(whole * group, live, place_one, 0)
    amount = 1
    while amount <= slots:

        @pl.when(lax.rem(lax.div(live, amount), 2) == 1)
        def arrived():
            some = adj_ref.at[0, 0, pl.ds(0, amount)]
            pltpu.make_async_copy(some, some, sem).wait()

        amount *= 2


def spread(adj_tiles, coord, count, target_count, source_count):
    tile = adj_tiles.shape[-1]
    shape = (source_count, target_count * tile, tile)
    return pl.pallas_call(
        functools.partial(spread_kernel, source_count=source_count, tile=tile),
        out_shape=jax.ShapeDtypeStruct(shape, jnp.bfloat16),
        in_specs=[pl.BlockSpec(memory_space=pltpu.SMEM)] * 2
        + [pl.BlockSpec(memory_space=pltpu.HBM)],
        out_specs=pl.BlockSpec(memory_space=pltpu.VMEM),
        scratch_shapes=[pltpu.SemaphoreType.DMA(())],
        compiler_params=pltpu.CompilerParams(vmem_limit_bytes=VMEM_GRANT),
        cost_estimate=pl.CostEstimate(
            flops=0, bytes_accessed=12 * 1024 * 1024, transcendentals=0
        ),
    )(
        pltpu.with_memory_space_constraint(coord, pltpu.HBM),
        count,
        pltpu.with_memory_space_constraint(adj_tiles, pltpu.HBM),
    )


def multiply_kernel(dense, *refs, spots, across, scale, added):
    base_ref = refs[0] if added else None
    piece_refs = refs[added : added + len(spots)]
    out_ref, feats, total = refs[added + len(spots) :]
    half = (lax.axis_index("z") + across) % 2
    own_y = lax.axis_index("y")
    turn = 1 - 2 * (lax.axis_index("row") % 2)
    y_size, z_count, rows, width = feats.shape
    tile = dense.shape[-1]
    per_z = y_size * rows // tile
    for ref, offset in zip(piece_refs, spots):
        feats[(own_y + turn * offset + y_size) % y_size] = ref[...]
    per_step = 4
    for at in range(0, z_count, per_step):
        left, right = [], []
        for z in range(at, at + per_step):
            left += [dense[(2 * z + half) * per_z + k] for k in range(per_z)]
            right += [feats[k, z] for k in range(y_size)]
        product = jnp.dot(
            jnp.concatenate(left, axis=1),
            jnp.concatenate(right, axis=0),
            preferred_element_type=jnp.float32,
        )
        if at > 0:
            product += total[...]
        elif added:
            product += base_ref[...]
        if at + per_step < z_count:
            total[...] = product
        else:
            out_ref[...] = (product * scale).astype(out_ref.dtype)


def multiply(dense, pieces, spots, across, kind, scale=1.0, base=None):
    z_count, rows, width = pieces[0].shape
    added = 0 if base is None else 1
    arrays = [dense] + ([base] if added else []) + pieces
    shape = (dense.shape[1], width)
    return pl.pallas_call(
        functools.partial(
            multiply_kernel, spots=spots, across=across, scale=scale, added=added
        ),
        out_shape=jax.ShapeDtypeStruct(shape, kind),
        in_specs=[pl.BlockSpec(memory_space=pltpu.VMEM)] * len(arrays),
        out_specs=pl.BlockSpec(memory_space=pltpu.VMEM),
        scratch_shapes=[
            pltpu.VMEM((len(spots), z_count, rows, width), jnp.bfloat16),
            pltpu.VMEM(shape, jnp.float32),
        ],
        compiler_params=pltpu.CompilerParams(vmem_limit_bytes=VMEM_GRANT),
        cost_estimate=pl.CostEstimate(
            flops=2 * dense.shape[1] * z_count * len(spots) * rows * width,
            bytes_accessed=6 * 1024 * 1024,
            transcendentals=0,
        ),
    )(*arrays)


def on_device(features, adj_tiles, tile_coord, tile_count, weight):
    tile = adj_tiles.shape[-1]
    rows, width = features.shape
    z_size, y_size = lax.axis_size("z"), lax.axis_size("y")
    row_size = lax.axis_size("row")
    target_count = rows * row_size // tile
    source_count = rows * z_size * y_size // tile
    half_z = z_size // 2
    groups = [[i + 2 * j for j in range(half_z)] for i in range(2)]
    own = lax.all_gather(features, "z", axis=0, axis_index_groups=groups)
    spots = [1, y_size - 1, 2, 0]
    near = [ring_shift(own, "y", -spot) for spot in spots[:-1]] + [own]
    far = [ring_shift(piece, "z", (-1) ** at) for at, piece in enumerate(near)]

    dense = spread(adj_tiles, tile_coord, tile_count, target_count, source_count)
    first = multiply(dense, near, spots, 0, jnp.float32)
    partial_value = multiply(dense, far, spots, 1, jnp.float32, SENT_SCALE, first)
    parts = lax.all_to_all(
        partial_value.astype(jnp.float16).reshape(row_size, rows, width), "row", 0, 0, tiled=True
    )
    hidden = jnp.sum(parts.astype(jnp.float32), axis=0) / SENT_SCALE
    hidden = hidden.astype(jnp.bfloat16)
    mixed = jnp.dot(hidden, weight, preferred_element_type=jnp.float32)
    return jax.nn.relu(mixed).astype(jnp.bfloat16)


def solution(mesh):
    devices = mesh.devices
    split = Mesh(
        devices.reshape(devices.shape[0], devices.shape[1] // Y_RING, Y_RING),
        ("row", "z", "y"),
    )
    col = ("z", "y")
    return jax.shard_map(
        on_device,
        mesh=split,
        in_specs=(
            P(("row", "z", "y"), None),
            P("row", col, None, None, None),
            P("row", col, None),
            P("row", col),
            P(),
        ),
        out_specs=P(("z", "y", "row"), None),
        check_vma=False,
    )
```

```python
import functools

import jax
import jax.numpy as jnp
from jax import lax
from jax.experimental import pallas as pl
from jax.experimental.pallas import tpu as pltpu
from jax.sharding import Mesh, PartitionSpec as P

Y_RING = 4
VMEM_GRANT = 24 * 1024 * 1024
SENT_SCALE = 16.0


def shift(value, z_step, y_step):
    axes = ("row", "z", "y")
    rows, z_size, y_size = (lax.axis_size(axis) for axis in axes)
    pairs = []
    for row in range(rows):
        turn = (-1) ** row
        for z in range(z_size):
            for y in range(y_size):
                to_z, to_y = (z + turn * z_step) % z_size, (y + turn * y_step) % y_size
                pairs.append(
                    ((row * z_size + z) * y_size + y, (row * z_size + to_z) * y_size + to_y)
                )
    return lax.ppermute(value, axes, pairs)


def spread_kernel(coord_ref, count_ref, adj_ref, dense, sem, *, source_count, tile):
    slots = adj_ref.shape[2]
    group = 8

    def clear(index, carry):
        dense[index] = jnp.zeros(dense.shape[1:], dense.dtype)
        return carry

    lax.fori_loop(0, source_count, clear, 0)
    live = count_ref[0, 0]

    def place(slot):
        spot = coord_ref[0, 0, slot]
        target = lax.div(spot, source_count)
        source = lax.rem(spot, source_count)
        rows = pl.ds(pl.multiple_of(target * tile, tile), tile)
        pltpu.make_async_copy(adj_ref.at[0, 0, slot], dense.at[source, rows], sem).start()

    def place_group(at, carry):
        for i in range(group):
            place(at * group + i)
        return carry

    def place_one(slot, carry):
        place(slot)
        return carry

    whole = lax.div(live, group)
    lax.fori_loop(0, whole, place_group, 0)
    lax.fori_loop(whole * group, live, place_one, 0)
    amount = 1
    while amount <= slots:

        @pl.when(lax.rem(lax.div(live, amount), 2) == 1)
        def arrived():
            some = adj_ref.at[0, 0, pl.ds(0, amount)]
            pltpu.make_async_copy(some, some, sem).wait()

        amount *= 2


def spread(adj_tiles, coord, count, target_count, source_count):
    tile = adj_tiles.shape[-1]
    shape = (source_count, target_count * tile, tile)
    return pl.pallas_call(
        functools.partial(spread_kernel, source_count=source_count, tile=tile),
        out_shape=jax.ShapeDtypeStruct(shape, jnp.bfloat16),
        in_specs=[pl.BlockSpec(memory_space=pltpu.SMEM)] * 2
        + [pl.BlockSpec(memory_space=pltpu.HBM)],
        out_specs=pl.BlockSpec(memory_space=pltpu.VMEM),
        scratch_shapes=[pltpu.SemaphoreType.DMA(())],
        compiler_params=pltpu.CompilerParams(vmem_limit_bytes=VMEM_GRANT),
        cost_estimate=pl.CostEstimate(
            flops=0, bytes_accessed=12 * 1024 * 1024, transcendentals=0
        ),
    )(
        pltpu.with_memory_space_constraint(coord, pltpu.HBM),
        count,
        pltpu.with_memory_space_constraint(adj_tiles, pltpu.HBM),
    )


def multiply_kernel(dense, *refs, spots, across, scale, added):
    base_ref = refs[0] if added else None
    piece_refs = refs[added : added + len(spots)]
    out_ref, feats, total = refs[added + len(spots) :]
    half = (lax.axis_index("z") + across) % 2
    own_y = lax.axis_index("y")
    turn = 1 - 2 * (lax.axis_index("row") % 2)
    y_size, z_count, rows, width = feats.shape
    tile = dense.shape[-1]
    per_z = y_size * rows // tile
    for ref, offset in zip(piece_refs, spots):
        feats[(own_y + turn * offset + y_size) % y_size] = ref[...]
    per_step = 4
    for at in range(0, z_count, per_step):
        left, right = [], []
        for z in range(at, at + per_step):
            left += [dense[(2 * z + half) * per_z + k] for k in range(per_z)]
            right += [feats[k, z] for k in range(y_size)]
        product = jnp.dot(
            jnp.concatenate(left, axis=1),
            jnp.concatenate(right, axis=0),
            preferred_element_type=jnp.float32,
        )
        if at > 0:
            product += total[...]
        elif added:
            product += base_ref[...]
        if at + per_step < z_count:
            total[...] = product
        else:
            out_ref[...] = (product * scale).astype(out_ref.dtype)


def multiply(dense, pieces, spots, across, kind, scale=1.0, base=None):
    z_count, rows, width = pieces[0].shape
    added = 0 if base is None else 1
    arrays = [dense] + ([base] if added else []) + pieces
    shape = (dense.shape[1], width)
    return pl.pallas_call(
        functools.partial(
            multiply_kernel, spots=spots, across=across, scale=scale, added=added
        ),
        out_shape=jax.ShapeDtypeStruct(shape, kind),
        in_specs=[pl.BlockSpec(memory_space=pltpu.VMEM)] * len(arrays),
        out_specs=pl.BlockSpec(memory_space=pltpu.VMEM),
        scratch_shapes=[
            pltpu.VMEM((len(spots), z_count, rows, width), jnp.bfloat16),
            pltpu.VMEM(shape, jnp.float32),
        ],
        compiler_params=pltpu.CompilerParams(vmem_limit_bytes=VMEM_GRANT),
        cost_estimate=pl.CostEstimate(
            flops=2 * dense.shape[1] * z_count * len(spots) * rows * width,
            bytes_accessed=6 * 1024 * 1024,
            transcendentals=0,
        ),
    )(*arrays)


def on_device(features, adj_tiles, tile_coord, tile_count, weight):
    tile = adj_tiles.shape[-1]
    rows, width = features.shape
    z_size, y_size = lax.axis_size("z"), lax.axis_size("y")
    row_size = lax.axis_size("row")
    target_count = rows * row_size // tile
    source_count = rows * z_size * y_size // tile
    half_z = z_size // 2
    groups = [[i + 2 * j for j in range(half_z)] for i in range(2)]
    own = lax.all_gather(features, "z", axis=0, axis_index_groups=groups)
    spots = [2, 1, y_size - 1, 0]
    opposite, one, other = (shift(own, 0, -spot) for spot in spots[:-1])
    near = [opposite, one, other, own]
    far = [
        shift(opposite, 1, 0),
        shift(one, -1, 0),
        shift(own, 1, -spots[2]),
        shift(own, -1, 0),
    ]

    dense = spread(adj_tiles, tile_coord, tile_count, target_count, source_count)
    first = multiply(dense, near, spots, 0, jnp.float32)
    partial_value = multiply(dense, far, spots, 1, jnp.float32, SENT_SCALE, first)
    parts = lax.all_to_all(
        partial_value.astype(jnp.float16).reshape(row_size, rows, width), "row", 0, 0, tiled=True
    )
    hidden = jnp.sum(parts.astype(jnp.float32), axis=0) / SENT_SCALE
    hidden = hidden.astype(jnp.bfloat16)
    mixed = jnp.dot(hidden, weight, preferred_element_type=jnp.float32)
    return jax.nn.relu(mixed).astype(jnp.bfloat16)


def solution(mesh):
    devices = mesh.devices
    split = Mesh(
        devices.reshape(devices.shape[0], devices.shape[1] // Y_RING, Y_RING),
        ("row", "z", "y"),
    )
    col = ("z", "y")
    return jax.shard_map(
        on_device,
        mesh=split,
        in_specs=(
            P(("row", "z", "y"), None),
            P("row", col, None, None, None),
            P("row", col, None),
            P("row", col),
            P(),
        ),
        out_specs=P(("z", "y", "row"), None),
        check_vma=False,
    )
```

```python
import functools

import jax
import jax.numpy as jnp
from jax import lax
from jax.experimental import pallas as pl
from jax.experimental.pallas import tpu as pltpu
from jax.sharding import Mesh, PartitionSpec as P

Y_RING = 4
VMEM_GRANT = 24 * 1024 * 1024
SENT_SCALE = 16.0


def ring_shift(value, axis, step):
    rows, size = lax.axis_size("row"), lax.axis_size(axis)
    pairs = [
        (row * size + i, row * size + (i + (-1) ** row * step) % size)
        for row in range(rows)
        for i in range(size)
    ]
    return lax.ppermute(value, ("row", axis), pairs)


def spread_kernel(coord_ref, count_ref, adj_ref, dense, sem, *, source_count, tile):
    slots = adj_ref.shape[2]
    group = 8

    def clear(index, carry):
        dense[index] = jnp.zeros(dense.shape[1:], dense.dtype)
        return carry

    lax.fori_loop(0, source_count, clear, 0)
    live = count_ref[0, 0]

    def place(slot):
        spot = coord_ref[0, 0, slot]
        target = lax.div(spot, source_count)
        source = lax.rem(spot, source_count)
        rows = pl.ds(pl.multiple_of(target * tile, tile), tile)
        pltpu.make_async_copy(adj_ref.at[0, 0, slot], dense.at[source, rows], sem).start()

    def place_group(at, carry):
        for i in range(group):
            place(at * group + i)
        return carry

    def place_one(slot, carry):
        place(slot)
        return carry

    whole = lax.div(live, group)
    lax.fori_loop(0, whole, place_group, 0)
    lax.fori_loop(whole * group, live, place_one, 0)
    amount = 1
    while amount <= slots:

        @pl.when(lax.rem(lax.div(live, amount), 2) == 1)
        def arrived():
            some = adj_ref.at[0, 0, pl.ds(0, amount)]
            pltpu.make_async_copy(some, some, sem).wait()

        amount *= 2


def spread(adj_tiles, coord, count, target_count, source_count):
    tile = adj_tiles.shape[-1]
    shape = (source_count, target_count * tile, tile)
    return pl.pallas_call(
        functools.partial(spread_kernel, source_count=source_count, tile=tile),
        out_shape=jax.ShapeDtypeStruct(shape, jnp.bfloat16),
        in_specs=[pl.BlockSpec(memory_space=pltpu.SMEM)] * 2
        + [pl.BlockSpec(memory_space=pltpu.HBM)],
        out_specs=pl.BlockSpec(memory_space=pltpu.VMEM),
        scratch_shapes=[pltpu.SemaphoreType.DMA(())],
        compiler_params=pltpu.CompilerParams(vmem_limit_bytes=VMEM_GRANT),
        cost_estimate=pl.CostEstimate(
            flops=0, bytes_accessed=12 * 1024 * 1024, transcendentals=0
        ),
    )(
        pltpu.with_memory_space_constraint(coord, pltpu.HBM),
        count,
        pltpu.with_memory_space_constraint(adj_tiles, pltpu.HBM),
    )


def multiply_kernel(dense, *refs, spots, across, scale, added):
    base_ref = refs[0] if added else None
    piece_refs = refs[added : added + len(spots)]
    out_ref, feats, total = refs[added + len(spots) :]
    half = (lax.axis_index("z") + across) % 2
    own_y = lax.axis_index("y")
    turn = 1 - 2 * (lax.axis_index("row") % 2)
    y_size, z_count, rows, width = feats.shape
    tile = dense.shape[-1]
    per_z = y_size * rows // tile
    for ref, offset in zip(piece_refs, spots):
        feats[(own_y + turn * offset + y_size) % y_size] = ref[...]
    per_step = 4
    for at in range(0, z_count, per_step):
        left, right = [], []
        for z in range(at, at + per_step):
            left += [dense[(2 * z + half) * per_z + k] for k in range(per_z)]
            right += [feats[k, z] for k in range(y_size)]
        product = jnp.dot(
            jnp.concatenate(left, axis=1),
            jnp.concatenate(right, axis=0),
            preferred_element_type=jnp.float32,
        )
        if at > 0:
            product += total[...]
        elif added:
            product += base_ref[...]
        if at + per_step < z_count:
            total[...] = product
        else:
            out_ref[...] = (product * scale).astype(out_ref.dtype)


def multiply(dense, pieces, spots, across, kind, scale=1.0, base=None):
    z_count, rows, width = pieces[0].shape
    added = 0 if base is None else 1
    arrays = [dense] + ([base] if added else []) + pieces
    shape = (dense.shape[1], width)
    return pl.pallas_call(
        functools.partial(
            multiply_kernel, spots=spots, across=across, scale=scale, added=added
        ),
        out_shape=jax.ShapeDtypeStruct(shape, kind),
        in_specs=[pl.BlockSpec(memory_space=pltpu.VMEM)] * len(arrays),
        out_specs=pl.BlockSpec(memory_space=pltpu.VMEM),
        scratch_shapes=[
            pltpu.VMEM((len(spots), z_count, rows, width), jnp.bfloat16),
            pltpu.VMEM(shape, jnp.float32),
        ],
        compiler_params=pltpu.CompilerParams(vmem_limit_bytes=VMEM_GRANT),
        cost_estimate=pl.CostEstimate(
            flops=2 * dense.shape[1] * z_count * len(spots) * rows * width,
            bytes_accessed=6 * 1024 * 1024,
            transcendentals=0,
        ),
    )(*arrays)


def on_device(features, adj_tiles, tile_coord, tile_count, weight):
    tile = adj_tiles.shape[-1]
    rows, width = features.shape
    z_size, y_size = lax.axis_size("z"), lax.axis_size("y")
    row_size = lax.axis_size("row")
    target_count = rows * row_size // tile
    source_count = rows * z_size * y_size // tile
    half_z = z_size // 2
    groups = [[i + 2 * j for j in range(half_z)] for i in range(2)]
    own = lax.all_gather(features, "z", axis=0, axis_index_groups=groups)
    spots = [2, 1, y_size - 1, 0]
    near = [ring_shift(own, "y", -spot) for spot in spots[:-1]] + [own]
    far = [ring_shift(piece, "z", (-1) ** at) for at, piece in enumerate(near[:-1])]
    late, _ = lax.optimization_barrier((own, far[0]))
    far.append(ring_shift(late, "z", -1))

    dense = spread(adj_tiles, tile_coord, tile_count, target_count, source_count)
    first = multiply(dense, near, spots, 0, jnp.float32)
    partial_value = multiply(dense, far, spots, 1, jnp.float32, SENT_SCALE, first)
    parts = lax.all_to_all(
        partial_value.astype(jnp.float16).reshape(row_size, rows, width), "row", 0, 0, tiled=True
    )
    hidden = jnp.sum(parts.astype(jnp.float32), axis=0) / SENT_SCALE
    hidden = hidden.astype(jnp.bfloat16)
    mixed = jnp.dot(hidden, weight, preferred_element_type=jnp.float32)
    return jax.nn.relu(mixed).astype(jnp.bfloat16)


def solution(mesh):
    devices = mesh.devices
    split = Mesh(
        devices.reshape(devices.shape[0], devices.shape[1] // Y_RING, Y_RING),
        ("row", "z", "y"),
    )
    col = ("z", "y")
    return jax.shard_map(
        on_device,
        mesh=split,
        in_specs=(
            P(("row", "z", "y"), None),
            P("row", col, None, None, None),
            P("row", col, None),
            P("row", col),
            P(),
        ),
        out_specs=P(("z", "y", "row"), None),
        check_vma=False,
    )
```

```python
import functools

import jax
import jax.numpy as jnp
from jax import lax
from jax.experimental import pallas as pl
from jax.experimental.pallas import tpu as pltpu
from jax.sharding import Mesh, PartitionSpec as P

Y_RING = 4
VMEM_GRANT = 24 * 1024 * 1024
SENT_SCALE = 16.0


def ring_shift(value, axis, step):
    rows, size = lax.axis_size("row"), lax.axis_size(axis)
    pairs = [
        (row * size + i, row * size + (i + (-1) ** row * step) % size)
        for row in range(rows)
        for i in range(size)
    ]
    return lax.ppermute(value, ("row", axis), pairs)


def spread_kernel(coord_ref, count_ref, adj_ref, dense, sem, *, source_count, tile):
    slots = adj_ref.shape[2]
    group = 8

    def clear(index, carry):
        dense[index] = jnp.zeros(dense.shape[1:], dense.dtype)
        return carry

    lax.fori_loop(0, source_count, clear, 0)
    live = count_ref[0, 0]

    def place(slot):
        spot = coord_ref[0, 0, slot]
        target = lax.div(spot, source_count)
        source = lax.rem(spot, source_count)
        rows = pl.ds(pl.multiple_of(target * tile, tile), tile)
        pltpu.make_async_copy(adj_ref.at[0, 0, slot], dense.at[source, rows], sem).start()

    def place_group(at, carry):
        for i in range(group):
            place(at * group + i)
        return carry

    def place_one(slot, carry):
        place(slot)
        return carry

    whole = lax.div(live, group)
    lax.fori_loop(0, whole, place_group, 0)
    lax.fori_loop(whole * group, live, place_one, 0)
    amount = 1
    while amount <= slots:

        @pl.when(lax.rem(lax.div(live, amount), 2) == 1)
        def arrived():
            some = adj_ref.at[0, 0, pl.ds(0, amount)]
            pltpu.make_async_copy(some, some, sem).wait()

        amount *= 2


def spread(adj_tiles, coord, count, target_count, source_count):
    tile = adj_tiles.shape[-1]
    shape = (source_count, target_count * tile, tile)
    return pl.pallas_call(
        functools.partial(spread_kernel, source_count=source_count, tile=tile),
        out_shape=jax.ShapeDtypeStruct(shape, jnp.bfloat16),
        in_specs=[pl.BlockSpec(memory_space=pltpu.SMEM)] * 2
        + [pl.BlockSpec(memory_space=pltpu.HBM)],
        out_specs=pl.BlockSpec(memory_space=pltpu.VMEM),
        scratch_shapes=[pltpu.SemaphoreType.DMA(())],
        compiler_params=pltpu.CompilerParams(vmem_limit_bytes=VMEM_GRANT),
        cost_estimate=pl.CostEstimate(
            flops=0, bytes_accessed=12 * 1024 * 1024, transcendentals=0
        ),
    )(
        pltpu.with_memory_space_constraint(coord, pltpu.HBM),
        count,
        pltpu.with_memory_space_constraint(adj_tiles, pltpu.HBM),
    )


def multiply_kernel(dense, *refs, spots, across, scale, added):
    base_ref = refs[0] if added else None
    piece_refs = refs[added : added + len(spots)]
    out_ref, feats, total = refs[added + len(spots) :]
    half = (lax.axis_index("z") + across) % 2
    own_y = lax.axis_index("y")
    turn = 1 - 2 * (lax.axis_index("row") % 2)
    y_size, z_count, rows, width = feats.shape
    tile = dense.shape[-1]
    per_z = y_size * rows // tile
    for ref, offset in zip(piece_refs, spots):
        feats[(own_y + turn * offset + y_size) % y_size] = ref[...]
    per_step = 4
    for at in range(0, z_count, per_step):
        left, right = [], []
        for z in range(at, at + per_step):
            left += [dense[(2 * z + half) * per_z + k] for k in range(per_z)]
            right += [feats[k, z] for k in range(y_size)]
        product = jnp.dot(
            jnp.concatenate(left, axis=1),
            jnp.concatenate(right, axis=0),
            preferred_element_type=jnp.float32,
        )
        if at > 0:
            product += total[...]
        elif added:
            product += base_ref[...]
        if at + per_step < z_count:
            total[...] = product
        else:
            out_ref[...] = (product * scale).astype(out_ref.dtype)


def multiply(dense, pieces, spots, across, kind, scale=1.0, base=None):
    z_count, rows, width = pieces[0].shape
    added = 0 if base is None else 1
    arrays = [dense] + ([base] if added else []) + pieces
    shape = (dense.shape[1], width)
    return pl.pallas_call(
        functools.partial(
            multiply_kernel, spots=spots, across=across, scale=scale, added=added
        ),
        out_shape=jax.ShapeDtypeStruct(shape, kind),
        in_specs=[pl.BlockSpec(memory_space=pltpu.VMEM)] * len(arrays),
        out_specs=pl.BlockSpec(memory_space=pltpu.VMEM),
        scratch_shapes=[
            pltpu.VMEM((len(spots), z_count, rows, width), jnp.bfloat16),
            pltpu.VMEM(shape, jnp.float32),
        ],
        compiler_params=pltpu.CompilerParams(vmem_limit_bytes=VMEM_GRANT),
        cost_estimate=pl.CostEstimate(
            flops=2 * dense.shape[1] * z_count * len(spots) * rows * width,
            bytes_accessed=6 * 1024 * 1024,
            transcendentals=0,
        ),
    )(*arrays)


def on_device(features, adj_tiles, tile_coord, tile_count, weight):
    tile = adj_tiles.shape[-1]
    rows, width = features.shape
    z_size, y_size = lax.axis_size("z"), lax.axis_size("y")
    row_size = lax.axis_size("row")
    target_count = rows * row_size // tile
    source_count = rows * z_size * y_size // tile
    half_z = z_size // 2
    groups = [[i + 2 * j for j in range(half_z)] for i in range(2)]
    own = lax.all_gather(features, "z", axis=0, axis_index_groups=groups)
    spots = [2, 1, y_size - 1, 0]
    across = ring_shift(own, "z", -1)
    opposite, one, other = (ring_shift(own, "y", -spot) for spot in spots[:-1])
    near = [opposite, one, other, own]
    far = [
        ring_shift(opposite, "z", 1),
        ring_shift(one, "z", -1),
        ring_shift(across, "y", -spots[2]),
        across,
    ]

    dense = spread(adj_tiles, tile_coord, tile_count, target_count, source_count)
    first = multiply(dense, near, spots, 0, jnp.float32)
    partial_value = multiply(dense, far, spots, 1, jnp.float32, SENT_SCALE, first)
    parts = lax.all_to_all(
        partial_value.astype(jnp.float16).reshape(row_size, rows, width), "row", 0, 0, tiled=True
    )
    hidden = jnp.sum(parts.astype(jnp.float32), axis=0) / SENT_SCALE
    hidden = hidden.astype(jnp.bfloat16)
    mixed = jnp.dot(hidden, weight, preferred_element_type=jnp.float32)
    return jax.nn.relu(mixed).astype(jnp.bfloat16)


def solution(mesh):
    devices = mesh.devices
    split = Mesh(
        devices.reshape(devices.shape[0], devices.shape[1] // Y_RING, Y_RING),
        ("row", "z", "y"),
    )
    col = ("z", "y")
    return jax.shard_map(
        on_device,
        mesh=split,
        in_specs=(
            P(("row", "z", "y"), None),
            P("row", col, None, None, None),
            P("row", col, None),
            P("row", col),
            P(),
        ),
        out_specs=P(("z", "y", "row"), None),
        check_vma=False,
    )
```
